32 devices in a mesh: mem: 4 (over z), lat: 2 (over x), lon: 4 (over y, core).
Axes of the slice: x: 2, y: 2, z: 4, core: 2. Of those that a mesh axis runs over, the one named last changes fastest.
Arguments:
- members: bfloat16 [8, 16, 128, 512], P('mem', None, 'lon', 'lat'), may hold values from -6 to 6
- control_fine: bfloat16 [8, 16, 128, 512], P('mem', None, 'lon', 'lat'), may hold values from -6 to 6
- control_mid: bfloat16 [8, 16, 64, 256], P('mem', None, 'lon', 'lat'), may hold values from -6 to 6
- control_coarse: bfloat16 [8, 16, 32, 128], P('mem', None, 'lon', 'lat'), may hold values from -6 to 6
- vertical: bfloat16 [3, 16, 16], replicated, may hold values from 0 to 0.25
- mid_picks: int32 [320], replicated, may hold values from 0 to 1
- coarse_picks: int32 [160], replicated, may hold values from 0 to 3
- band_radii: int32 [3], replicated, may hold values from 4 to 8
Outputs:
- increment: float32 [4, 512, 512], P('lon', 'mem', 'lat')
The draws below stay inside these ranges and needn't reach their ends.
Inputs may be any that keep to these rules, and one draw needn't show every extreme that they name: `mid_picks`: entry i of the first 256 entries picks fine row 2 i + entry for middle-band row i; entry j of the rest picks fine column 2 j + entry for middle-band column j. `coarse_picks`: entry i of the first 128 entries picks fine row 4 i + entry for coarse-band row i; entry j of the rest picks fine column 4 j + entry for coarse-band column j. `band_radii`: radius of each band's horizontal taper, in that band's cells.
All inputs are finite; a program needn't handle non-finite values.
Results may differ from the reference program's by a relative error of at most 0.0062.
Values may be sent and summed in bfloat16 or wider, within the bound.
A program may use at most 64 MiB of HBM per device.

```python
import math
import jax
import jax.numpy as jnp
from jax import lax

LEV = 16
REACH = 8
COLS_DEV = 32
MEMBERS = 8
NLAT = 512
NLON = 128
N_LON = 4


def set_ends(array, rng, low, top_value):
    shape = array.shape
    place = [jax.random.randint(jax.random.fold_in(rng, axis), (), 0, shape[axis]) for axis in range(len(shape))]
    array = array.at[tuple(place)].set(low)
    longest = shape.index(max(shape))
    place[longest] = (place[longest] + 1) % shape[longest]
    return array.at[tuple(place)].set(top_value)


def raised(entries, own_key, source, target, shards_of, factor):
    owner, partner = [(jnp.arange(entries.shape[dim]) // (entries.shape[dim] // shards_of)).reshape([-1 if axis == dim else 1 for axis in range(entries.ndim)]) for dim in (source, target)]
    chosen = jax.random.permutation(own_key, shards_of)[partner]
    strong = (owner == chosen) | (owner == (partner + shards_of // 2) % shards_of)
    return jnp.where(strong, factor * entries, entries)


def block_levels(own_key, extent, shards, smallest, high):
    factor_of = 1.0
    for position, blocks in shards:
        steps = jax.random.uniform(jax.random.fold_in(jax.random.fold_in(own_key, 6), position), (blocks,), jnp.float32, smallest / len(shards), high / len(shards))
        factor_of = factor_of * jnp.repeat(jnp.exp(steps), extent[position] // blocks).reshape((-1,) + (1,) * (len(extent) - 1 - position))
    return factor_of


def gaussian(stream_key, dims, scale, bound, split=(), kind=jnp.bfloat16):
    values = jax.random.normal(stream_key, dims, jnp.float32) * scale
    if len(split) > 0:
        values = block_levels(stream_key, dims, split, -0.22, 0.18) * values
    return jnp.clip(values, min=-bound, max=bound).astype(kind)


def bell_draw_with(stream_key, extent, scale, bound, shards, heavy, kind=jnp.bfloat16):
    drawn = scale * jax.random.normal(stream_key, extent, jnp.float32)
    if shards:
        drawn = drawn * block_levels(stream_key, extent, shards, -0.22, 0.18)
    return jnp.clip(raised(drawn, jax.random.fold_in(stream_key, 3), *heavy), -bound, bound).astype(kind)


def setup_inputs(seed: int = 0) -> dict:
    splits = jax.random.split(jax.random.key(seed), 9)
    return {
        "members": bell_draw_with(splits[0], (MEMBERS, LEV, NLON, NLAT), 1.0, 6.0, ((0, 4), (2, 4), (3, 2)), (0, 2, 4, 2.0)),
        "control_fine": gaussian(splits[1], (MEMBERS, LEV, NLON, NLAT), 1.0, 6.0, ((0, 4), (2, 4), (3, 2))),
        "control_mid": gaussian(splits[2], (MEMBERS, LEV, NLON // 2, NLAT // 2), 1.0, 6.0, ((0, 4), (2, 4), (3, 2))),
        "control_coarse": gaussian(splits[3], (MEMBERS, LEV, NLON // 4, NLAT // 4), 1.0, 6.0, ((0, 4), (2, 4), (3, 2))),
        "vertical": jnp.clip(jax.random.uniform(splits[4], (3, LEV, LEV), jnp.float32, 0.0, 0.25), 0.0, 0.25).astype(jnp.bfloat16),
        "mid_picks": set_ends(jax.random.randint(splits[5], (NLAT // 2 + NLON // 2,), 0, 2), jax.random.fold_in(splits[5], 1), 0, 1).astype(jnp.int32),
        "coarse_picks": set_ends(jax.random.randint(splits[6], (NLAT // 4 + NLON // 4,), 0, 4), jax.random.fold_in(splits[6], 1), 0, 3).astype(jnp.int32),
        "band_radii": jax.random.randint(splits[7], (3,), 4, 9).astype(jnp.int32),
    }


band_factors = (1, 2, 4)

def tap_weights(radius):
    offsets = jnp.arange(-REACH, REACH + 1).astype(jnp.float32)
    reach_now = radius.astype(jnp.float32)
    spread = 0.5 * reach_now
    unnormed = jnp.where(jnp.abs(offsets) <= reach_now, jnp.exp(-0.5 * jnp.square(offsets / spread)), jnp.float32(0.0))
    return (unnormed / jnp.sum(unnormed)).astype(jnp.bfloat16)

def localize(control, vertical_band, weights):
    mixed = jnp.einsum('kl,lcr->kcr', vertical_band.astype(jnp.float32), control.astype(jnp.float32), precision=lax.Precision.HIGHEST).astype(jnp.bfloat16)
    length = mixed.shape[2]
    padded = jnp.pad(mixed, ((0, 0), (0, 0), (REACH, REACH))).astype(jnp.float32)
    weight_wide = weights.astype(jnp.float32)
    across = jnp.zeros(mixed.shape, jnp.float32)
    for offset in range(2 * REACH + 1):
        across = across + weight_wide[offset] * padded[:, :, offset:offset + length]
    across = lax.optimization_barrier(across.astype(jnp.bfloat16)).astype(jnp.float32)
    width_cols = across.shape[1]
    wrapped = jnp.concatenate([across[:, width_cols - REACH:, :], across, across[:, :REACH, :]], axis=1)
    result = jnp.zeros(across.shape, jnp.float32)
    for offset in range(2 * REACH + 1):
        result = result + weight_wide[offset] * wrapped[:, offset:offset + width_cols, :]
    return result

def restrict(member, chosen, factor, row_total):
    band_rows = row_total // factor
    band_cols = chosen.shape[0] - band_rows
    row_pick = factor * jnp.arange(band_rows, dtype=jnp.int32) + chosen[:band_rows].astype(jnp.int32)
    col_pick = factor * jnp.arange(band_cols, dtype=jnp.int32) + chosen[band_rows:].astype(jnp.int32)
    return member[:, col_pick, :][:, :, row_pick]

def prolong(values, factor):
    return jnp.repeat(jnp.repeat(values, factor, axis=1), factor, axis=2)

def reference(members, control_fine, control_mid, control_coarse, vertical, mid_picks, coarse_picks, band_radii):
    member_total = members.shape[0]
    row_total = members.shape[3]
    chosen_all = (None, mid_picks, coarse_picks)
    weight_sets = [tap_weights(band_radii[band_index]) for band_index in range(3)]

    def add_member(accumulated, sliced):
        member = sliced[0]
        for band_index in range(3):
            factor = band_factors[band_index]
            filtered = localize(sliced[band_index + 1], vertical[band_index], weight_sets[band_index])
            if factor == 1:
                restricted = member
            else:
                restricted = restrict(member, chosen_all[band_index], factor, row_total)
            product = restricted.astype(jnp.float32) * filtered
            accumulated = accumulated + prolong(product, factor)
        return (accumulated, None)
    start = jnp.zeros((LEV, NLON, NLAT), jnp.float32)
    accumulated, unused = lax.scan(add_member, start, (members, control_fine, control_mid, control_coarse))
    field = accumulated / math.sqrt(member_total - 1)
    blocks = field.reshape(LEV, N_LON, COLS_DEV, NLAT).transpose(1, 0, 2, 3)
    return blocks.reshape(N_LON, LEV * COLS_DEV, NLAT)
```

```python
import functools
import math

import jax
import jax.numpy as jnp
from jax import lax
from jax.experimental import pallas as pl
from jax.experimental.pallas import tpu as pltpu
from jax.sharding import PartitionSpec as P

REACH = 8
FACTORS = (1, 2, 4)
MESH = pl.DeviceIdType.MESH
F32 = jnp.float32
BF16 = jnp.bfloat16


def log2(value):
    shift = value.bit_length() - 1
    assert value == 1 << shift
    return shift


def iota(shape, dim):
    return lax.broadcasted_iota(jnp.int32, shape, dim)


def dot(left, right):
    return jnp.dot(left, right, preferred_element_type=F32)


def dot_nt(left, right):
    return lax.dot_general(left, right, (((1,), (1,)), ((), ())), preferred_element_type=F32)


def dot_tn(left, right):
    return lax.dot_general(left, right, (((0,), (0,)), ((), ())), preferred_element_type=F32)


def one_hot(condition):
    return jnp.where(condition, 1.0, 0.0).astype(BF16)


def flat(cells):
    lanes = cells.shape[-1]
    if cells.shape[-2] % 16 == 0:
        return cells.reshape(-1, lanes)
    return cells.astype(F32).reshape(-1, lanes).astype(BF16)


def taper(radius, distance):
    reach_now = radius.astype(F32)
    spread = 0.5 * reach_now

    def raw(offset):
        offset = offset.astype(F32)
        return jnp.where(
            jnp.abs(offset) <= reach_now, jnp.exp(-0.5 * jnp.square(offset / spread)), 0.0
        )

    lane = iota((1, 128), 1)
    each = jnp.where(lane <= 2 * REACH, raw(lane - REACH), 0.0)
    total = jnp.sum(each, axis=1, keepdims=True)
    return raw(distance) / total


def pick_vector(picks_ref, start, rows, period):
    picks = picks_ref[...].astype(F32)
    length = picks.shape[1]
    place = iota((rows, length), 0)
    index = start + (place if period == rows else place & (period - 1))
    hit = iota((rows, length), 1) == index
    return jnp.sum(jnp.where(hit, picks, 0.0), axis=1, keepdims=True)


def kernel(
    sizes,
    members_hbm,
    fine_hbm,
    mid_hbm,
    coarse_hbm,
    vertical_ref,
    mid_picks_ref,
    coarse_picks_ref,
    radii_ref,
    out_ref,
    members_ref,
    own0,
    own1,
    own2,
    side0,
    side1,
    side2,
    strip_out,
    strip_in,
    corner_out,
    corner_in,
    field_ref,
    sum_out,
    sum_in,
    load_sem,
    lon_send,
    lon_recv,
    strip_send,
    strip_recv,
    corner_send,
    corner_recv,
    sum_send,
    sum_recv,
):
    n_mem, n_lat, n_lon, shifts = sizes
    mem, lat, lon = lax.axis_index("mem"), lax.axis_index("lat"), lax.axis_index("lon")
    count, levels, cols, rows = members_ref.shape
    controls_hbm = (fine_hbm, mid_hbm, coarse_hbm)
    owns = (own0, own1, own2)
    sides = (side0, side1, side2)
    band_cols = [cols // f for f in FACTORS]
    band_rows = [rows // f for f in FACTORS]
    after, before = lax.rem(lon + 1, n_lon), lax.rem(lon + n_lon - 1, n_lon)

    loads = [
        pltpu.make_async_copy(src, dst, load_sem.at[i])
        for i, (src, dst) in enumerate(zip(controls_hbm + (members_hbm,), owns + (members_ref,)))
    ]
    for load in loads:
        load.start()

    partners = [{"lon": before}, {"lon": after}]
    for s in shifts:
        there = lax.rem(lat + s, n_lat)
        partners += [{"lat": there}, {"lat": there, "lon": before}, {"lat": there, "lon": after}]
    for s in range(1, n_mem):
        partners.append({"mem": lax.rem(mem + s, n_mem)})
    barrier = pltpu.get_barrier_semaphore()
    for partner in partners:
        pl.semaphore_signal(barrier, inc=1, device_id=partner, device_id_type=MESH)
    pl.semaphore_wait(barrier, len(partners))

    def remote(src, dst, send, recv, device):
        return pltpu.make_async_remote_copy(
            src_ref=src, dst_ref=dst, send_sem=send, recv_sem=recv, device_id=device, device_id_type=MESH
        )

    lon_copies = []
    for b in range(3):
        width = band_cols[b]
        lon_copies.append(
            remote(
                controls_hbm[b].at[:, :, width - REACH : width, :],
                sides[b].at[:, 0],
                lon_send.at[2 * b],
                lon_recv.at[2 * b],
                {"lon": after},
            )
        )
        lon_copies.append(
            remote(
                controls_hbm[b].at[:, :, 0:REACH, :],
                sides[b].at[:, 1],
                lon_send.at[2 * b + 1],
                lon_recv.at[2 * b + 1],
                {"lon": before},
            )
        )
    for copy in lon_copies:
        copy.start()

    starts = []
    place = 0
    for b in range(3):
        starts.append(place)
        place += count * levels * band_cols[b]
    lat_copies = []
    for b in range(3):
        loads[b].wait()
    for b in range(3):
        length = band_rows[b]
        h = iota((2 * REACH, length), 0)
        i = iota((2 * REACH, length), 1)
        edge = one_hot(i == jnp.where(h < REACH, h, length - 2 * REACH + h))
        width = count * levels * band_cols[b]
        strip_out[:, starts[b] : starts[b] + width] = dot_nt(edge, flat(owns[b][...])).astype(BF16)
        near = owns[b][...].astype(F32)
        for side in range(2):
            first = 0 if side == 0 else band_cols[b] - REACH
            part = near[:, :, first : first + REACH, :].reshape(-1, length).astype(BF16)
            packed = dot_nt(edge, part).astype(BF16)
            for m in range(count):
                lanes = levels * REACH
                corner_out[side, b * count + m] = packed[:, m * lanes : (m + 1) * lanes]
    for k, s in enumerate(shifts):
        slot = shifts.index((n_lat - s) % n_lat)
        there = lax.rem(lat + s, n_lat)
        lat_copies.append(
            remote(strip_out, strip_in.at[slot], strip_send.at[slot], strip_recv.at[slot], {"lat": there})
        )
        for side in range(2):
            target = before if side == 0 else after
            lat_copies.append(
                remote(
                    corner_out.at[side],
                    corner_in.at[slot, :, 1 - side],
                    corner_send.at[2 * slot + side],
                    corner_recv.at[2 * slot + side],
                    {"lat": there, "lon": target},
                )
            )
    for copy in lat_copies:
        copy.start()

    row_own, row_edge, kron_own, kron_side = [], [], [], []
    for b in range(3):
        radius = radii_ref[b]
        length, width = band_rows[b], band_cols[b]
        shape = (length, length)
        row_own.append(taper(radius, iota(shape, 0) - iota(shape, 1)).astype(BF16))
        shape = (2 * REACH, length)
        h, i = iota(shape, 0), iota(shape, 1)
        edge_weights = taper(radius, jnp.where(h < REACH, length + h - i, h - 2 * REACH - i))
        edges = []
        for s in shifts:
            head_ok = jnp.where(lat + 1 < n_lat, 1.0, 0.0) if s == 1 else 0.0
            tail_ok = jnp.where(lat > 0, 1.0, 0.0) if s == n_lat - 1 else 0.0
            edges.append((edge_weights * jnp.where(h < REACH, head_ok, tail_ok)).astype(BF16))
        row_edge.append(edges)

        tall = levels * width
        c_shift, l_mask = log2(width), levels - 1
        pick_level = one_hot((iota((tall, levels), 0) >> c_shift) == iota((tall, levels), 1))
        pick_col = one_hot((iota((tall, width), 0) & (width - 1)) == iota((tall, width), 1))
        by_level = dot(pick_level, vertical_ref[b]).astype(BF16)

        def kron(weights, source_level, source_place):
            left = dot(by_level, source_level)
            right = dot(dot(pick_col, weights.astype(BF16)).astype(BF16), source_place)
            return (left * right).astype(BF16)

        shape = (width, width)
        own_weights = taper(radius, iota(shape, 1) - iota(shape, 0))
        level_of = one_hot(iota((levels, tall), 0) == (iota((levels, tall), 1) >> c_shift))
        place_of = one_hot(iota((width, tall), 0) == (iota((width, tall), 1) & (width - 1)))
        kron_own.append(kron(own_weights, level_of, place_of))
        shape = (width, 2 * REACH)
        c, q = iota(shape, 0), iota(shape, 1)
        side_weights = taper(radius, jnp.where(q < REACH, q - REACH - c, width + q - REACH - c))
        wide = 2 * levels * REACH
        r_shift = log2(REACH)
        level_of = one_hot(
            iota((levels, wide), 0) == ((iota((levels, wide), 1) >> r_shift) & l_mask)
        )
        spot = iota((2 * REACH, wide), 1)
        spot = ((spot >> log2(levels * REACH)) << r_shift) + (spot & (REACH - 1))
        place_of = one_hot(iota((2 * REACH, wide), 0) == spot)
        kron_side.append(kron(side_weights, level_of, place_of))

    loads[3].wait()
    member_cells = flat(members_ref[...])
    group = max(1, min(levels, 256 // cols))
    restricted = [None]
    for b in (1, 2):
        factor = FACTORS[b]
        picks_ref = mid_picks_ref if b == 1 else coarse_picks_ref
        length, width = band_rows[b], band_cols[b]
        row_pick = pick_vector(picks_ref, lat * length, length, length)
        target = (iota((length, rows), 0) * factor).astype(F32) + row_pick
        by_rows = dot_nt(member_cells, one_hot(iota((length, rows), 1).astype(F32) == target)).astype(BF16)
        tall = group * width
        col_pick = pick_vector(picks_ref, n_lat * length + lon * width, tall, width)
        target = (iota((tall, group * cols), 0) * factor).astype(F32) + col_pick
        chooser = one_hot(iota((tall, group * cols), 1).astype(F32) == target)
        pieces = []
        for m in range(count):
            parts = []
            for g in range(levels // group):
                first = (m * levels + g * group) * cols
                parts.append(dot(chooser, by_rows[first : first + group * cols]))
            pieces.append(jnp.concatenate(parts, axis=0))
        restricted.append(pieces)

    own_filtered = [dot(flat(owns[b][...]), row_own[b]) for b in range(3)]
    for copy in lat_copies:
        copy.wait_recv()
    local = []
    for b in range(3):
        tall = levels * band_cols[b]
        across = own_filtered[b]
        for k in range(len(shifts)):
            strip = strip_in[k, :, starts[b] : starts[b] + count * tall]
            across = across + dot_tn(strip, row_edge[b][k])
        across = across.astype(BF16)
        local.append([dot(kron_own[b], across[m * tall : (m + 1) * tall]) for m in range(count)])

    for copy in lon_copies:
        copy.wait_recv()
    wide = 2 * levels * REACH
    sums = []
    for b in range(3):
        halo = dot(flat(sides[b][...]), row_own[b])
        total = None
        for m in range(count):
            across = halo[m * wide : (m + 1) * wide]
            for k in range(len(shifts)):
                corner = jnp.concatenate(
                    [corner_in[k, b * count + m, 0], corner_in[k, b * count + m, 1]], axis=1
                )
                across = across + dot_tn(corner, row_edge[b][k])
            filtered = local[b][m] + dot(kron_side[b], across.astype(BF16))
            if b == 0:
                member = flat(members_ref[m]).astype(F32)
            else:
                member = restricted[b][m]
            product = member * filtered
            total = product if total is None else total + product
        sums.append(total)

    field = [sums[0][g * group * cols : (g + 1) * group * cols] for g in range(levels // group)]
    for b in (1, 2):
        f_shift = log2(FACTORS[b])
        length, width = band_rows[b], band_cols[b]
        repeat = one_hot(iota((length, rows), 0) == (iota((length, rows), 1) >> f_shift))
        spread = dot(sums[b].astype(BF16), repeat).astype(BF16)
        tall = group * width
        shape = (group * cols, tall)
        repeat = one_hot((iota(shape, 0) >> f_shift) == iota(shape, 1))
        for g in range(levels // group):
            field[g] = field[g] + dot(repeat, spread[g * tall : (g + 1) * tall])
    whole = jnp.concatenate(field, axis=0)
    block = levels * cols // n_mem
    field_ref[...] = whole.reshape(n_mem, block, rows)
    sum_out[...] = whole.reshape(n_mem, block, rows).astype(BF16)

    sum_copies = []
    for s in range(1, n_mem):
        there = lax.rem(mem + s, n_mem)
        sum_copies.append(
            remote(
                sum_out.at[there],
                sum_in.at[s - 1],
                sum_send.at[s - 1],
                sum_recv.at[s - 1],
                {"mem": there},
            )
        )
    for copy in sum_copies:
        copy.start()
    total = field_ref[mem]
    for s, copy in enumerate(sum_copies):
        copy.wait_recv()
        total = total + sum_in[s].astype(F32)
    out_ref[...] = total
    for copy in lon_copies + lat_copies + sum_copies:
        copy.wait_send()


def on_device(
    members,
    control_fine,
    control_mid,
    control_coarse,
    vertical,
    mid_picks,
    coarse_picks,
    band_radii,
):
    n_mem, n_lat, n_lon = (lax.axis_size(axis) for axis in ("mem", "lat", "lon"))
    shifts = sorted({1, n_lat - 1}) if n_lat > 1 else []
    slots = max(1, len(shifts))
    count, levels, cols, rows = members.shape
    controls = (control_fine, control_mid, control_coarse)
    block = levels * cols // n_mem
    strip_lanes = sum(count * levels * c.shape[2] for c in controls)
    corner_lanes = levels * REACH
    any_spec = pl.BlockSpec(memory_space=pl.ANY)
    vmem_spec = pl.BlockSpec(memory_space=pltpu.VMEM)
    dma = pltpu.SemaphoreType.DMA
    scratch = (
        [pltpu.VMEM(members.shape, BF16)]
        + [pltpu.VMEM(c.shape, BF16) for c in controls]
        + [pltpu.VMEM((count, 2, levels, REACH, c.shape[3]), BF16) for c in controls]
        + [
            pltpu.VMEM((2 * REACH, strip_lanes), BF16),
            pltpu.VMEM((slots, 2 * REACH, strip_lanes), BF16),
            pltpu.VMEM((2, 3 * count, 2 * REACH, corner_lanes), BF16),
            pltpu.VMEM((slots, 3 * count, 2, 2 * REACH, corner_lanes), BF16),
            pltpu.VMEM((n_mem, block, rows), F32),
            pltpu.VMEM((n_mem, block, rows), BF16),
            pltpu.VMEM((n_mem, block, rows), BF16),
            dma((4,)),
            dma((6,)),
            dma((6,)),
            dma((slots,)),
            dma((slots,)),
            dma((2 * slots,)),
            dma((2 * slots,)),
            dma((n_mem,)),
            dma((n_mem,)),
        ]
    )
    summed = pl.pallas_call(
        functools.partial(kernel, (n_mem, n_lat, n_lon, shifts)),
        out_shape=jax.ShapeDtypeStruct((block, rows), F32),
        in_specs=[any_spec] * 4 + [vmem_spec] * 3 + [pl.BlockSpec(memory_space=pltpu.SMEM)],
        out_specs=vmem_spec,
        scratch_shapes=scratch,
        compiler_params=pltpu.CompilerParams(
            collective_id=0, has_side_effects=True, vmem_limit_bytes=48 << 20
        ),
    )(
        *((members,) + controls),
        vertical,
        mid_picks[None, :],
        coarse_picks[None, :],
        band_radii,
    )
    scale = 1.0 / math.sqrt(count * n_mem - 1)
    return (summed * scale)[None, :, :]


def solution(mesh):
    placed = (
        P("mem", None, "lon", "lat"),
        P("mem", None, "lon", "lat"),
        P("mem", None, "lon", "lat"),
        P("mem", None, "lon", "lat"),
        P(),
        P(),
        P(),
        P(),
    )
    return jax.shard_map(
        on_device, mesh=mesh, in_specs=placed, out_specs=P("lon", "mem", "lat"), check_vma=False
    )
```

```python
import functools
import math

import jax
import jax.numpy as jnp
from jax import lax
from jax.experimental import pallas as pl
from jax.experimental.pallas import tpu as pltpu
from jax.sharding import PartitionSpec as P

REACH = 8
FACTORS = (1, 2, 4)
MESH = pl.DeviceIdType.MESH
F32 = jnp.float32
BF16 = jnp.bfloat16


def log2(value):
    shift = value.bit_length() - 1
    assert value == 1 << shift
    return shift


def iota(shape, dim):
    return lax.broadcasted_iota(jnp.int32, shape, dim)


def dot(left, right):
    return jnp.dot(left, right, preferred_element_type=F32)


def dot_nt(left, right):
    return lax.dot_general(left, right, (((1,), (1,)), ((), ())), preferred_element_type=F32)


def dot_tn(left, right):
    return lax.dot_general(left, right, (((0,), (0,)), ((), ())), preferred_element_type=F32)


def one_hot(condition):
    return jnp.where(condition, 1.0, 0.0).astype(BF16)


def flat(cells):
    lanes = cells.shape[-1]
    if cells.shape[-2] % 16 == 0:
        return cells.reshape(-1, lanes)
    return cells.astype(F32).reshape(-1, lanes).astype(BF16)


def taper(radius, distance):
    reach_now = radius.astype(F32)
    spread = 0.5 * reach_now

    def raw(offset):
        offset = offset.astype(F32)
        return jnp.where(
            jnp.abs(offset) <= reach_now, jnp.exp(-0.5 * jnp.square(offset / spread)), 0.0
        )

    lane = iota((1, 128), 1)
    each = jnp.where(lane <= 2 * REACH, raw(lane - REACH), 0.0)
    total = jnp.sum(each, axis=1, keepdims=True)
    return raw(distance) / total


def pick_vector(picks_ref, start, rows, period):
    picks = picks_ref[...].astype(F32)
    length = picks.shape[1]
    place = iota((rows, length), 0)
    index = start + (place if period == rows else place & (period - 1))
    hit = iota((rows, length), 1) == index
    return jnp.sum(jnp.where(hit, picks, 0.0), axis=1, keepdims=True)


def kernel(
    sizes,
    members_hbm,
    fine_hbm,
    mid_hbm,
    coarse_hbm,
    vertical_hbm,
    mid_picks_hbm,
    coarse_picks_hbm,
    radii_hbm,
    out_ref,
    vertical_ref,
    mid_picks_ref,
    coarse_picks_ref,
    radii_ref,
    members_ref,
    own0,
    own1,
    own2,
    side0,
    side1,
    side2,
    strip_out,
    strip_in,
    corner_out,
    corner_in,
    field_ref,
    sum_out,
    sum_in,
    load_sem,
    lon_send,
    lon_recv,
    strip_send,
    strip_recv,
    corner_send,
    corner_recv,
    sum_send,
    sum_recv,
):
    n_mem, n_lat, n_lon, shifts = sizes
    mem, lat, lon = lax.axis_index("mem"), lax.axis_index("lat"), lax.axis_index("lon")
    count, levels, cols, rows = members_ref.shape
    controls_hbm = (fine_hbm, mid_hbm, coarse_hbm)
    owns = (own0, own1, own2)
    sides = (side0, side1, side2)
    band_cols = [cols // f for f in FACTORS]
    band_rows = [rows // f for f in FACTORS]
    after, before = lax.rem(lon + 1, n_lon), lax.rem(lon + n_lon - 1, n_lon)

    loads = [
        pltpu.make_async_copy(src, dst, load_sem.at[i])
        for i, (src, dst) in enumerate(zip(controls_hbm + (members_hbm,), owns + (members_ref,)))
    ]
    tables = [
        pltpu.make_async_copy(src, dst, load_sem.at[4 + i])
        for i, (src, dst) in enumerate(
            (
                (radii_hbm, radii_ref),
                (vertical_hbm, vertical_ref),
                (mid_picks_hbm, mid_picks_ref.at[0]),
                (coarse_picks_hbm, coarse_picks_ref.at[0]),
            )
        )
    ]
    for load in tables + loads:
        load.start()

    partners = [{"lon": before}, {"lon": after}]
    for s in shifts:
        there = lax.rem(lat + s, n_lat)
        partners += [{"lat": there}, {"lat": there, "lon": before}, {"lat": there, "lon": after}]
    for s in range(1, n_mem):
        partners.append({"mem": lax.rem(mem + s, n_mem)})
    barrier = pltpu.get_barrier_semaphore()
    for partner in partners:
        pl.semaphore_signal(barrier, inc=1, device_id=partner, device_id_type=MESH)
    pl.semaphore_wait(barrier, len(partners))

    def remote(src, dst, send, recv, device):
        return pltpu.make_async_remote_copy(
            src_ref=src, dst_ref=dst, send_sem=send, recv_sem=recv, device_id=device, device_id_type=MESH
        )

    lon_copies = []
    for b in range(3):
        width = band_cols[b]
        lon_copies.append(
            remote(
                controls_hbm[b].at[:, :, width - REACH : width, :],
                sides[b].at[:, 0],
                lon_send.at[2 * b],
                lon_recv.at[2 * b],
                {"lon": after},
            )
        )
        lon_copies.append(
            remote(
                controls_hbm[b].at[:, :, 0:REACH, :],
                sides[b].at[:, 1],
                lon_send.at[2 * b + 1],
                lon_recv.at[2 * b + 1],
                {"lon": before},
            )
        )
    for copy in lon_copies:
        copy.start()

    starts = []
    place = 0
    for b in range(3):
        starts.append(place)
        place += count * levels * band_cols[b]
    lat_copies = []
    for b in range(3):
        loads[b].wait()
    for b in range(3):
        length = band_rows[b]
        h = iota((2 * REACH, length), 0)
        i = iota((2 * REACH, length), 1)
        edge = one_hot(i == jnp.where(h < REACH, h, length - 2 * REACH + h))
        width = count * levels * band_cols[b]
        strip_out[:, starts[b] : starts[b] + width] = dot_nt(edge, flat(owns[b][...])).astype(BF16)
        near = owns[b][...].astype(F32)
        for side in range(2):
            first = 0 if side == 0 else band_cols[b] - REACH
            part = near[:, :, first : first + REACH, :].reshape(-1, length).astype(BF16)
            packed = dot_nt(edge, part).astype(BF16)
            for m in range(count):
                lanes = levels * REACH
                corner_out[side, b * count + m] = packed[:, m * lanes : (m + 1) * lanes]
    for k, s in enumerate(shifts):
        slot = shifts.index((n_lat - s) % n_lat)
        there = lax.rem(lat + s, n_lat)
        lat_copies.append(
            remote(strip_out, strip_in.at[slot], strip_send.at[slot], strip_recv.at[slot], {"lat": there})
        )
        for side in range(2):
            target = before if side == 0 else after
            lat_copies.append(
                remote(
                    corner_out.at[side],
                    corner_in.at[slot, :, 1 - side],
                    corner_send.at[2 * slot + side],
                    corner_recv.at[2 * slot + side],
                    {"lat": there, "lon": target},
                )
            )
    for copy in lat_copies:
        copy.start()

    for load in tables:
        load.wait()
    row_own, row_edge, kron_own, kron_side = [], [], [], []
    for b in range(3):
        radius = radii_ref[b]
        length, width = band_rows[b], band_cols[b]
        shape = (length, length)
        row_own.append(taper(radius, iota(shape, 0) - iota(shape, 1)).astype(BF16))
        shape = (2 * REACH, length)
        h, i = iota(shape, 0), iota(shape, 1)
        edge_weights = taper(radius, jnp.where(h < REACH, length + h - i, h - 2 * REACH - i))
        edges = []
        for s in shifts:
            head_ok = jnp.where(lat + 1 < n_lat, 1.0, 0.0) if s == 1 else 0.0
            tail_ok = jnp.where(lat > 0, 1.0, 0.0) if s == n_lat - 1 else 0.0
            edges.append((edge_weights * jnp.where(h < REACH, head_ok, tail_ok)).astype(BF16))
        row_edge.append(edges)

        tall = levels * width
        c_shift, l_mask = log2(width), levels - 1
        pick_level = one_hot((iota((tall, levels), 0) >> c_shift) == iota((tall, levels), 1))
        pick_col = one_hot((iota((tall, width), 0) & (width - 1)) == iota((tall, width), 1))
        by_level = dot(pick_level, vertical_ref[b]).astype(BF16)

        def kron(weights, source_level, source_place):
            left = dot(by_level, source_level)
            right = dot(dot(pick_col, weights.astype(BF16)).astype(BF16), source_place)
            return (left * right).astype(BF16)

        shape = (width, width)
        own_weights = taper(radius, iota(shape, 1) - iota(shape, 0))
        level_of = one_hot(iota((levels, tall), 0) == (iota((levels, tall), 1) >> c_shift))
        place_of = one_hot(iota((width, tall), 0) == (iota((width, tall), 1) & (width - 1)))
        kron_own.append(kron(own_weights, level_of, place_of))
        shape = (width, 2 * REACH)
        c, q = iota(shape, 0), iota(shape, 1)
        side_weights = taper(radius, jnp.where(q < REACH, q - REACH - c, width + q - REACH - c))
        wide = 2 * levels * REACH
        r_shift = log2(REACH)
        level_of = one_hot(
            iota((levels, wide), 0) == ((iota((levels, wide), 1) >> r_shift) & l_mask)
        )
        spot = iota((2 * REACH, wide), 1)
        spot = ((spot >> log2(levels * REACH)) << r_shift) + (spot & (REACH - 1))
        place_of = one_hot(iota((2 * REACH, wide), 0) == spot)
        kron_side.append(kron(side_weights, level_of, place_of))

    loads[3].wait()
    member_cells = flat(members_ref[...])
    group = max(1, min(levels, 256 // cols))
    restricted = [None]
    for b in (1, 2):
        factor = FACTORS[b]
        picks_ref = mid_picks_ref if b == 1 else coarse_picks_ref
        length, width = band_rows[b], band_cols[b]
        row_pick = pick_vector(picks_ref, lat * length, length, length)
        target = (iota((length, rows), 0) * factor).astype(F32) + row_pick
        by_rows = dot_nt(member_cells, one_hot(iota((length, rows), 1).astype(F32) == target)).astype(BF16)
        tall = group * width
        col_pick = pick_vector(picks_ref, n_lat * length + lon * width, tall, width)
        target = (iota((tall, group * cols), 0) * factor).astype(F32) + col_pick
        chooser = one_hot(iota((tall, group * cols), 1).astype(F32) == target)
        pieces = []
        for m in range(count):
            parts = []
            for g in range(levels // group):
                first = (m * levels + g * group) * cols
                parts.append(dot(chooser, by_rows[first : first + group * cols]))
            pieces.append(jnp.concatenate(parts, axis=0))
        restricted.append(pieces)

    own_filtered = [dot(flat(owns[b][...]), row_own[b]) for b in range(3)]
    for copy in lat_copies:
        copy.wait_recv()
    local = []
    for b in range(3):
        tall = levels * band_cols[b]
        across = own_filtered[b]
        for k in range(len(shifts)):
            strip = strip_in[k, :, starts[b] : starts[b] + count * tall]
            across = across + dot_tn(strip, row_edge[b][k])
        across = across.astype(BF16)
        local.append([dot(kron_own[b], across[m * tall : (m + 1) * tall]) for m in range(count)])

    for copy in lon_copies:
        copy.wait_recv()
    wide = 2 * levels * REACH
    sums = []
    for b in range(3):
        halo = dot(flat(sides[b][...]), row_own[b])
        total = None
        for m in range(count):
            across = halo[m * wide : (m + 1) * wide]
            for k in range(len(shifts)):
                corner = jnp.concatenate(
                    [corner_in[k, b * count + m, 0], corner_in[k, b * count + m, 1]], axis=1
                )
                across = across + dot_tn(corner, row_edge[b][k])
            filtered = local[b][m] + dot(kron_side[b], across.astype(BF16))
            if b == 0:
                member = flat(members_ref[m]).astype(F32)
            else:
                member = restricted[b][m]
            product = member * filtered
            total = product if total is None else total + product
        sums.append(total)

    field = [sums[0][g * group * cols : (g + 1) * group * cols] for g in range(levels // group)]
    for b in (1, 2):
        f_shift = log2(FACTORS[b])
        length, width = band_rows[b], band_cols[b]
        repeat = one_hot(iota((length, rows), 0) == (iota((length, rows), 1) >> f_shift))
        spread = dot(sums[b].astype(BF16), repeat).astype(BF16)
        tall = group * width
        shape = (group * cols, tall)
        repeat = one_hot((iota(shape, 0) >> f_shift) == iota(shape, 1))
        for g in range(levels // group):
            field[g] = field[g] + dot(repeat, spread[g * tall : (g + 1) * tall])
    whole = jnp.concatenate(field, axis=0)
    block = levels * cols // n_mem
    field_ref[...] = whole.reshape(n_mem, block, rows)
    sum_out[...] = whole.reshape(n_mem, block, rows).astype(BF16)

    sum_copies = []
    for s in range(1, n_mem):
        there = lax.rem(mem + s, n_mem)
        sum_copies.append(
            remote(
                sum_out.at[there],
                sum_in.at[s - 1],
                sum_send.at[s - 1],
                sum_recv.at[s - 1],
                {"mem": there},
            )
        )
    for copy in sum_copies:
        copy.start()
    total = field_ref[mem]
    for s, copy in enumerate(sum_copies):
        copy.wait_recv()
        total = total + sum_in[s].astype(F32)
    out_ref[...] = total
    for copy in lon_copies + lat_copies + sum_copies:
        copy.wait_send()


def on_device(
    members,
    control_fine,
    control_mid,
    control_coarse,
    vertical,
    mid_picks,
    coarse_picks,
    band_radii,
):
    n_mem, n_lat, n_lon = (lax.axis_size(axis) for axis in ("mem", "lat", "lon"))
    shifts = sorted({1, n_lat - 1}) if n_lat > 1 else []
    slots = max(1, len(shifts))
    count, levels, cols, rows = members.shape
    controls = (control_fine, control_mid, control_coarse)
    block = levels * cols // n_mem
    strip_lanes = sum(count * levels * c.shape[2] for c in controls)
    corner_lanes = levels * REACH
    hbm_spec = pl.BlockSpec(memory_space=pltpu.HBM)
    vmem_spec = pl.BlockSpec(memory_space=pltpu.VMEM)
    dma = pltpu.SemaphoreType.DMA
    scratch = (
        [
            pltpu.VMEM(vertical.shape, BF16),
            pltpu.VMEM((1,) + mid_picks.shape, jnp.int32),
            pltpu.VMEM((1,) + coarse_picks.shape, jnp.int32),
            pltpu.SMEM(band_radii.shape, jnp.int32),
            pltpu.VMEM(members.shape, BF16),
        ]
        + [pltpu.VMEM(c.shape, BF16) for c in controls]
        + [pltpu.VMEM((count, 2, levels, REACH, c.shape[3]), BF16) for c in controls]
        + [
            pltpu.VMEM((2 * REACH, strip_lanes), BF16),
            pltpu.VMEM((slots, 2 * REACH, strip_lanes), BF16),
            pltpu.VMEM((2, 3 * count, 2 * REACH, corner_lanes), BF16),
            pltpu.VMEM((slots, 3 * count, 2, 2 * REACH, corner_lanes), BF16),
            pltpu.VMEM((n_mem, block, rows), F32),
            pltpu.VMEM((n_mem, block, rows), BF16),
            pltpu.VMEM((n_mem, block, rows), BF16),
            dma((8,)),
            dma((6,)),
            dma((6,)),
            dma((slots,)),
            dma((slots,)),
            dma((2 * slots,)),
            dma((2 * slots,)),
            dma((n_mem,)),
            dma((n_mem,)),
        ]
    )
    summed = pl.pallas_call(
        functools.partial(kernel, (n_mem, n_lat, n_lon, shifts)),
        out_shape=jax.ShapeDtypeStruct((block, rows), F32),
        in_specs=[hbm_spec] * 8,
        out_specs=vmem_spec,
        scratch_shapes=scratch,
        compiler_params=pltpu.CompilerParams(
            collective_id=0, has_side_effects=True, vmem_limit_bytes=67043328
        ),
    )(
        *((members,) + controls),
        vertical,
        mid_picks,
        coarse_picks,
        band_radii,
    )
    scale = 1.0 / math.sqrt(count * n_mem - 1)
    return (summed * scale)[None, :, :]


def solution(mesh):
    placed = (
        P("mem", None, "lon", "lat"),
        P("mem", None, "lon", "lat"),
        P("mem", None, "lon", "lat"),
        P("mem", None, "lon", "lat"),
        P(),
        P(),
        P(),
        P(),
    )
    return jax.shard_map(
        on_device, mesh=mesh, in_specs=placed, out_specs=P("lon", "mem", "lat"), check_vma=False
    )
```

```python
import functools
import math

import jax
import jax.numpy as jnp
from jax import lax
from jax.experimental import pallas as pl
from jax.experimental.pallas import tpu as pltpu
from jax.sharding import PartitionSpec as P

REACH = 8
FACTORS = (1, 2, 4)
MESH = pl.DeviceIdType.MESH
F32 = jnp.float32
BF16 = jnp.bfloat16


def log2(value):
    shift = value.bit_length() - 1
    assert value == 1 << shift
    return shift


def iota(shape, dim):
    return lax.broadcasted_iota(jnp.int32, shape, dim)


def dot(left, right):
    return jnp.dot(left, right, preferred_element_type=F32)


def dot_nt(left, right):
    return lax.dot_general(left, right, (((1,), (1,)), ((), ())), preferred_element_type=F32)


def dot_tn(left, right):
    return lax.dot_general(left, right, (((0,), (0,)), ((), ())), preferred_element_type=F32)


def one_hot(condition):
    return jnp.where(condition, 1.0, 0.0).astype(BF16)


def flat(cells):
    lanes = cells.shape[-1]
    if cells.shape[-2] % 16 == 0:
        return cells.reshape(-1, lanes)
    return cells.astype(F32).reshape(-1, lanes).astype(BF16)


def taper(radius, distance):
    reach_now = radius.astype(F32)
    spread = 0.5 * reach_now

    def raw(offset):
        offset = offset.astype(F32)
        return jnp.where(
            jnp.abs(offset) <= reach_now, jnp.exp(-0.5 * jnp.square(offset / spread)), 0.0
        )

    lane = iota((1, 128), 1)
    each = jnp.where(lane <= 2 * REACH, raw(lane - REACH), 0.0)
    total = jnp.sum(each, axis=1, keepdims=True)
    return raw(distance) / total


def pick_vector(picks_ref, start, rows, period):
    picks = picks_ref[...].astype(F32)
    length = picks.shape[1]
    place = iota((rows, length), 0)
    index = start + (place if period == rows else place & (period - 1))
    hit = iota((rows, length), 1) == index
    return jnp.sum(jnp.where(hit, picks, 0.0), axis=1, keepdims=True)


def kernel(
    sizes,
    members_hbm,
    fine_hbm,
    mid_hbm,
    coarse_hbm,
    vertical_hbm,
    mid_picks_hbm,
    coarse_picks_hbm,
    radii_hbm,
    out_ref,
    vertical_ref,
    mid_picks_ref,
    coarse_picks_ref,
    radii_ref,
    members_ref,
    own0,
    own1,
    own2,
    side0,
    side1,
    side2,
    strip_out,
    strip_in,
    corner_out,
    corner_in,
    *rest,

):
    n_mem, n_lat, n_lon, shifts, parts = sizes
    field_refs, sum_outs, sum_ins = (
        rest[i * len(parts) : (i + 1) * len(parts)] for i in range(3)
    )
    load_sem, lon_send, lon_recv, strip_send, strip_recv = rest[3 * len(parts) :][:5]
    corner_send, corner_recv, sum_send, sum_recv = rest[3 * len(parts) :][5:]
    mem, lat, lon = lax.axis_index("mem"), lax.axis_index("lat"), lax.axis_index("lon")
    count, levels, cols, rows = members_ref.shape
    controls_hbm = (fine_hbm, mid_hbm, coarse_hbm)
    owns = (own0, own1, own2)
    sides = (side0, side1, side2)
    band_cols = [cols // f for f in FACTORS]
    band_rows = [rows // f for f in FACTORS]
    after, before = lax.rem(lon + 1, n_lon), lax.rem(lon + n_lon - 1, n_lon)

    loads = [
        pltpu.make_async_copy(src, dst, load_sem.at[i])
        for i, (src, dst) in enumerate(zip(controls_hbm + (members_hbm,), owns + (members_ref,)))
    ]
    tables = [
        pltpu.make_async_copy(src, dst, load_sem.at[4 + i])
        for i, (src, dst) in enumerate(
            (
                (radii_hbm, radii_ref),
                (vertical_hbm, vertical_ref),
                (mid_picks_hbm, mid_picks_ref.at[0]),
                (coarse_picks_hbm, coarse_picks_ref.at[0]),
            )
        )
    ]
    for load in tables + loads:
        load.start()

    partners = [{"lon": before}, {"lon": after}]
    for s in shifts:
        there = lax.rem(lat + s, n_lat)
        partners += [{"lat": there}, {"lat": there, "lon": before}, {"lat": there, "lon": after}]
    for s in range(1, n_mem):
        partners.append({"mem": lax.rem(mem + s, n_mem)})
    barrier = pltpu.get_barrier_semaphore()
    for partner in partners:
        pl.semaphore_signal(barrier, inc=1, device_id=partner, device_id_type=MESH)
    pl.semaphore_wait(barrier, len(partners))

    def remote(src, dst, send, recv, device):
        return pltpu.make_async_remote_copy(
            src_ref=src, dst_ref=dst, send_sem=send, recv_sem=recv, device_id=device, device_id_type=MESH
        )

    def sum_copy(p, s):
        there = lax.rem(mem + s, n_mem)
        return remote(
            sum_outs[p].at[there],
            sum_ins[p].at[s - 1],
            sum_send.at[p, s - 1],
            sum_recv.at[p, s - 1],
            {"mem": there},
        )

    def start_sum(p, dest):
        @pl.when(mem != dest)
        def _():
            slot = lax.rem(dest - mem + n_mem, n_mem) - 1
            remote(
                sum_outs[p].at[dest],
                sum_ins[p].at[slot],
                sum_send.at[p, slot],
                sum_recv.at[p, slot],
                {"mem": dest},
            ).start()

    lon_copies = []
    for b in range(3):
        width = band_cols[b]
        lon_copies.append(
            remote(
                controls_hbm[b].at[:, :, width - REACH : width, :],
                sides[b].at[:, 0],
                lon_send.at[2 * b],
                lon_recv.at[2 * b],
                {"lon": after},
            )
        )
        lon_copies.append(
            remote(
                controls_hbm[b].at[:, :, 0:REACH, :],
                sides[b].at[:, 1],
                lon_send.at[2 * b + 1],
                lon_recv.at[2 * b + 1],
                {"lon": before},
            )
        )
    for copy in lon_copies[4:] + lon_copies[2:4] + lon_copies[:2]:
        copy.start()

    starts = []
    place = 0
    for b in range(3):
        starts.append(place)
        place += count * levels * band_cols[b]
    lat_copies = []
    for b in range(3):
        loads[b].wait()
    for b in range(3):
        length = band_rows[b]
        h = iota((2 * REACH, length), 0)
        i = iota((2 * REACH, length), 1)
        edge = one_hot(i == jnp.where(h < REACH, h, length - 2 * REACH + h))
        width = count * levels * band_cols[b]
        strip_out[:, starts[b] : starts[b] + width] = dot_nt(edge, flat(owns[b][...])).astype(BF16)
        near = owns[b][...].astype(F32)
        for side in range(2):
            first = 0 if side == 0 else band_cols[b] - REACH
            part = near[:, :, first : first + REACH, :].reshape(-1, length).astype(BF16)
            packed = dot_nt(edge, part).astype(BF16)
            for m in range(count):
                lanes = levels * REACH
                corner_out[side, b * count + m] = packed[:, m * lanes : (m + 1) * lanes]
    for k, s in enumerate(shifts):
        slot = shifts.index((n_lat - s) % n_lat)
        there = lax.rem(lat + s, n_lat)
        lat_copies.append(
            remote(strip_out, strip_in.at[slot], strip_send.at[slot], strip_recv.at[slot], {"lat": there})
        )
        for side in range(2):
            target = before if side == 0 else after
            lat_copies.append(
                remote(
                    corner_out.at[side],
                    corner_in.at[slot, :, 1 - side],
                    corner_send.at[2 * slot + side],
                    corner_recv.at[2 * slot + side],
                    {"lat": there, "lon": target},
                )
            )
    for copy in lat_copies:
        copy.start()

    for load in tables:
        load.wait()
    row_own, row_edge, kron_own, kron_side = [], [], [], []
    for b in range(3):
        radius = radii_ref[b]
        length, width = band_rows[b], band_cols[b]
        shape = (length, length)
        row_own.append(taper(radius, iota(shape, 0) - iota(shape, 1)).astype(BF16))
        shape = (2 * REACH, length)
        h, i = iota(shape, 0), iota(shape, 1)
        edge_weights = taper(radius, jnp.where(h < REACH, length + h - i, h - 2 * REACH - i))
        edges = []
        for s in shifts:
            head_ok = jnp.where(lat + 1 < n_lat, 1.0, 0.0) if s == 1 else 0.0
            tail_ok = jnp.where(lat > 0, 1.0, 0.0) if s == n_lat - 1 else 0.0
            edges.append((edge_weights * jnp.where(h < REACH, head_ok, tail_ok)).astype(BF16))
        row_edge.append(edges)

        by_parts_own, by_parts_side = [], []
        tall = levels * width
        level_of = one_hot(iota((levels, tall), 0) == (iota((levels, tall), 1) >> log2(width)))
        place_of = one_hot(iota((width, tall), 0) == (iota((width, tall), 1) & (width - 1)))
        wide = 2 * levels * REACH
        r_shift = log2(REACH)
        side_level_of = one_hot(
            iota((levels, wide), 0) == ((iota((levels, wide), 1) >> r_shift) & (levels - 1))
        )
        spot = iota((2 * REACH, wide), 1)
        spot = ((spot >> log2(levels * REACH)) << r_shift) + (spot & (REACH - 1))
        side_place_of = one_hot(iota((2 * REACH, wide), 0) == spot)
        shape = (width, width)
        own_weights = taper(radius, iota(shape, 1) - iota(shape, 0)).astype(BF16)
        shape = (width, 2 * REACH)
        c, q = iota(shape, 0), iota(shape, 1)
        side_weights = jnp.where(q < REACH, q - REACH - c, width + q - REACH - c)
        side_weights = taper(radius, side_weights).astype(BF16)
        for part in parts if b == 0 else ("all",):
            part_width = width_of(part, width)
            tall = levels * part_width
            pick_level = one_hot(
                (iota((tall, levels), 0) >> log2(part_width)) == iota((tall, levels), 1)
            )
            column = column_of(part, iota((tall, width), 0) & (part_width - 1), width)
            pick_col = one_hot(column == iota((tall, width), 1))
            by_level = dot(pick_level, vertical_ref[b]).astype(BF16)

            def kron(weights, source_level, source_place):
                left = dot(by_level, source_level)
                right = dot(dot(pick_col, weights).astype(BF16), source_place)
                return (left * right).astype(BF16)

            by_parts_own.append(kron(own_weights, level_of, place_of))
            if part != "inner":
                by_parts_side.append(kron(side_weights, side_level_of, side_place_of))
            else:
                by_parts_side.append(None)
        kron_own.append(by_parts_own)
        kron_side.append(by_parts_side)

    loads[3].wait()
    member_cells = flat(members_ref[...])
    group = max(1, min(levels, 256 // cols))
    restricted = [None]
    for b in (1, 2):
        factor = FACTORS[b]
        picks_ref = mid_picks_ref if b == 1 else coarse_picks_ref
        length, width = band_rows[b], band_cols[b]
        row_pick = pick_vector(picks_ref, lat * length, length, length)
        target = (iota((length, rows), 0) * factor).astype(F32) + row_pick
        by_rows = dot_nt(member_cells, one_hot(iota((length, rows), 1).astype(F32) == target)).astype(BF16)
        tall = group * width
        col_pick = pick_vector(picks_ref, n_lat * length + lon * width, tall, width)
        target = (iota((tall, group * cols), 0) * factor).astype(F32) + col_pick
        chooser = one_hot(iota((tall, group * cols), 1).astype(F32) == target)
        pieces = []
        for m in range(count):
            picked = []
            for g in range(levels // group):
                first = (m * levels + g * group) * cols
                picked.append(dot(chooser, by_rows[first : first + group * cols]))
            pieces.append(jnp.concatenate(picked, axis=0))
        restricted.append(pieces)

    own_filtered = [dot(flat(owns[b][...]), row_own[b]) for b in range(3)]
    for copy in lat_copies:
        copy.wait_recv()
    local = []
    for b in range(3):
        tall = levels * band_cols[b]
        across = own_filtered[b]
        for k in range(len(shifts)):
            strip = strip_in[k, :, starts[b] : starts[b] + count * tall]
            across = across + dot_tn(strip, row_edge[b][k])
        across = across.astype(BF16)
        local.append(
            [
                [dot(part, across[m * tall : (m + 1) * tall]) for m in range(count)]
                for part in kron_own[b]
            ]
        )

    wide = 2 * levels * REACH

    def side_cells(b):
        for copy in lon_copies[2 * b : 2 * b + 2]:
            copy.wait_recv()
        halo = dot(flat(sides[b][...]), row_own[b])
        cells = []
        for m in range(count):
            across = halo[m * wide : (m + 1) * wide]
            for k in range(len(shifts)):
                corner = jnp.concatenate(
                    [corner_in[k, b * count + m, 0], corner_in[k, b * count + m, 1]], axis=1
                )
                across = across + dot_tn(corner, row_edge[b][k])
            cells.append(across.astype(BF16))
        return cells

    spread = [None]
    for b in (1, 2):
        cells = side_cells(b)
        total = None
        for m in range(count):
            product = restricted[b][m] * (local[b][0][m] + dot(kron_side[b][0], cells[m]))
            total = product if total is None else total + product
        length = band_rows[b]
        repeat = one_hot(iota((length, rows), 0) == (iota((length, rows), 1) >> log2(FACTORS[b])))
        spread.append(dot(total.astype(BF16), repeat).astype(BF16))

    block = levels * cols // n_mem
    sum_copies = []
    for p, part in enumerate(parts):
        part_width = width_of(part, cols)
        part_block = block * part_width // cols
        cells = None if part == "inner" else side_cells(0)
        fine = []
        for m in range(count):
            member = columns_of(part, members_ref[m].astype(F32))
            filtered = local[0][p][m]
            if cells is not None:
                filtered = filtered + dot(kron_side[0][p], cells[m])
            fine.append(member * filtered)
        total = fine[0]
        for product in fine[1:]:
            total = total + product
        tall = group * part_width
        dests = n_mem * group // levels
        for g in range(levels // group):
            piece = total[g * tall : (g + 1) * tall]
            for b in (1, 2):
                from_tall = group * band_cols[b]
                r = iota((tall, from_tall), 0)
                source = column_of(part, r & (part_width - 1), cols) >> log2(FACTORS[b])
                source = ((r >> log2(part_width)) << log2(band_cols[b])) + source
                repeat = one_hot(source == iota((tall, from_tall), 1))
                piece = piece + dot(repeat, spread[b][g * from_tall : (g + 1) * from_tall])
            piece = piece.reshape(-1, part_block, rows)
            here = slice(g * piece.shape[0], (g + 1) * piece.shape[0])
            field_refs[p][here] = piece
            sum_outs[p][here] = piece.astype(BF16)
            if levels // group == 1 or n_mem % (levels // group):
                continue
            for dest in range(g * dests, (g + 1) * dests):
                start_sum(p, dest)
        if levels // group == 1 or n_mem % (levels // group):
            for dest in range(n_mem):
                start_sum(p, dest)

    for p, part in enumerate(parts):
        total = field_refs[p][mem]
        for s in range(1, n_mem):
            sum_copy(p, s).wait_recv()
            total = total + sum_ins[p][s - 1].astype(F32)
        if part == "all":
            out_ref[0] = total
            continue
        total = total.reshape(block // cols, -1, rows)
        if part == "inner":
            out_ref[:, REACH : cols - REACH, :] = total
        else:
            out_ref[:, :REACH, :] = total[:, :REACH, :]
            out_ref[:, cols - REACH :, :] = total[:, REACH:, :]
    for copy in lon_copies + lat_copies:
        copy.wait_send()
    for p in range(len(parts)):
        for s in range(1, n_mem):
            sum_copy(p, s).wait_send()


def width_of(part, width):
    return {"inner": width - 2 * REACH, "outer": 2 * REACH, "all": width}[part]


def column_of(part, place, width):
    if part == "inner":
        return place + REACH
    if part == "outer":
        return jnp.where(place < REACH, place, place + (width - 2 * REACH))
    return place


def columns_of(part, cells):
    if part == "inner":
        cells = cells[:, REACH : cells.shape[1] - REACH, :]
    if part == "outer":
        cells = jnp.concatenate(
            [cells[:, :REACH, :], cells[:, cells.shape[1] - REACH :, :]], axis=1
        )
    return cells.reshape(-1, cells.shape[2])


def on_device(
    members,
    control_fine,
    control_mid,
    control_coarse,
    vertical,
    mid_picks,
    coarse_picks,
    band_radii,
):
    n_mem, n_lat, n_lon = (lax.axis_size(axis) for axis in ("mem", "lat", "lon"))
    shifts = sorted({1, n_lat - 1}) if n_lat > 1 else []
    slots = max(1, len(shifts))
    count, levels, cols, rows = members.shape
    controls = (control_fine, control_mid, control_coarse)
    block = levels * cols // n_mem
    inner = cols - 2 * REACH
    split = block % cols == 0 and inner > 0 and inner & (inner - 1) == 0
    parts = ("inner", "outer") if split else ("all",)
    out_shape = (block // cols, cols, rows) if split else (1, block, rows)
    strip_lanes = sum(count * levels * c.shape[2] for c in controls)
    corner_lanes = levels * REACH
    hbm_spec = pl.BlockSpec(memory_space=pltpu.HBM)
    vmem_spec = pl.BlockSpec(memory_space=pltpu.VMEM)
    dma = pltpu.SemaphoreType.DMA
    scratch = (
        [
            pltpu.VMEM(vertical.shape, BF16),
            pltpu.VMEM((1,) + mid_picks.shape, jnp.int32),
            pltpu.VMEM((1,) + coarse_picks.shape, jnp.int32),
            pltpu.SMEM(band_radii.shape, jnp.int32),
            pltpu.VMEM(members.shape, BF16),
        ]
        + [pltpu.VMEM(c.shape, BF16) for c in controls]
        + [pltpu.VMEM((count, 2, levels, REACH, c.shape[3]), BF16) for c in controls]
        + [
            pltpu.VMEM((2 * REACH, strip_lanes), BF16),
            pltpu.VMEM((slots, 2 * REACH, strip_lanes), BF16),
            pltpu.VMEM((2, 3 * count, 2 * REACH, corner_lanes), BF16),
            pltpu.VMEM((slots, 3 * count, 2, 2 * REACH, corner_lanes), BF16),
        ]
        + [pltpu.VMEM((n_mem, block * width_of(p, cols) // cols, rows), F32) for p in parts]
        + [pltpu.VMEM((n_mem, block * width_of(p, cols) // cols, rows), BF16) for p in parts] * 2
        + [
            dma((8,)),
            dma((6,)),
            dma((6,)),
            dma((slots,)),
            dma((slots,)),
            dma((2 * slots,)),
            dma((2 * slots,)),
            dma((len(parts), n_mem)),
            dma((len(parts), n_mem)),
        ]
    )
    summed = pl.pallas_call(
        functools.partial(kernel, (n_mem, n_lat, n_lon, shifts, parts)),
        out_shape=jax.ShapeDtypeStruct(out_shape, F32),
        in_specs=[hbm_spec] * 8,
        out_specs=vmem_spec,
        scratch_shapes=scratch,
        compiler_params=pltpu.CompilerParams(
            collective_id=0, has_side_effects=True, vmem_limit_bytes=67043328
        ),
    )(
        *((members,) + controls),
        vertical,
        mid_picks,
        coarse_picks,
        band_radii,
    )
    scale = 1.0 / math.sqrt(count * n_mem - 1)
    return (summed * scale).reshape(1, block, rows)


def solution(mesh):
    placed = (
        P("mem", None, "lon", "lat"),
        P("mem", None, "lon", "lat"),
        P("mem", None, "lon", "lat"),
        P("mem", None, "lon", "lat"),
        P(),
        P(),
        P(),
        P(),
    )
    return jax.shard_map(
        on_device, mesh=mesh, in_specs=placed, out_specs=P("lon", "mem", "lat"), check_vma=False
    )
```

```python
import functools
import math

import jax
import jax.numpy as jnp
from jax import lax
from jax.experimental import pallas as pl
from jax.experimental.pallas import tpu as pltpu
from jax.sharding import PartitionSpec as P

REACH = 8
FACTORS = (1, 2, 4)
MESH = pl.DeviceIdType.MESH
F32 = jnp.float32
BF16 = jnp.bfloat16


def log2(value):
    shift = value.bit_length() - 1
    assert value == 1 << shift
    return shift


def iota(shape, dim):
    return lax.broadcasted_iota(jnp.int32, shape, dim)


def dot(left, right):
    return jnp.dot(left, right, preferred_element_type=F32)


def dot_nt(left, right):
    return lax.dot_general(left, right, (((1,), (1,)), ((), ())), preferred_element_type=F32)


def dot_tn(left, right):
    return lax.dot_general(left, right, (((0,), (0,)), ((), ())), preferred_element_type=F32)


def one_hot(condition):
    return jnp.where(condition, 1.0, 0.0).astype(BF16)


def flat(cells):
    lanes = cells.shape[-1]
    if cells.shape[-2] % 16 == 0:
        return cells.reshape(-1, lanes)
    return cells.astype(F32).reshape(-1, lanes).astype(BF16)


def taper(radius, distance):
    reach_now = radius.astype(F32)
    spread = 0.5 * reach_now

    def raw(offset):
        offset = offset.astype(F32)
        return jnp.where(
            jnp.abs(offset) <= reach_now, jnp.exp(-0.5 * jnp.square(offset / spread)), 0.0
        )

    lane = iota((1, 128), 1)
    each = jnp.where(lane <= 2 * REACH, raw(lane - REACH), 0.0)
    total = jnp.sum(each, axis=1, keepdims=True)
    return raw(distance) / total


def pick_vector(picks_ref, start, rows, period):
    picks = picks_ref[...].astype(F32)
    length = picks.shape[1]
    place = iota((rows, length), 0)
    index = start + (place if period == rows else place & (period - 1))
    hit = iota((rows, length), 1) == index
    return jnp.sum(jnp.where(hit, picks, 0.0), axis=1, keepdims=True)


def kernel(
    sizes,
    members_hbm,
    fine_hbm,
    mid_hbm,
    coarse_hbm,
    vertical_hbm,
    mid_picks_hbm,
    coarse_picks_hbm,
    radii_hbm,
    out_ref,
    vertical_ref,
    mid_picks_ref,
    coarse_picks_ref,
    radii_ref,
    members_ref,
    own0,
    own1,
    own2,
    side0,
    side1,
    side2,
    strip_out,
    strip_in,
    corner_out,
    corner_in,
    *rest,

):
    n_mem, n_lat, n_lon, shifts, parts = sizes
    field_refs, sum_outs, sum_ins = (
        rest[i * len(parts) : (i + 1) * len(parts)] for i in range(3)
    )
    load_sem, lon_send, lon_recv, strip_send, strip_recv = rest[3 * len(parts) :][:5]
    corner_send, corner_recv, sum_send, sum_recv = rest[3 * len(parts) :][5:]
    mem, lat, lon = lax.axis_index("mem"), lax.axis_index("lat"), lax.axis_index("lon")
    count, levels, cols, rows = members_ref.shape
    controls_hbm = (fine_hbm, mid_hbm, coarse_hbm)
    owns = (own0, own1, own2)
    sides = (side0, side1, side2)
    band_cols = [cols // f for f in FACTORS]
    band_rows = [rows // f for f in FACTORS]
    after, before = lax.rem(lon + 1, n_lon), lax.rem(lon + n_lon - 1, n_lon)

    loads = [
        pltpu.make_async_copy(src, dst, load_sem.at[i])
        for i, (src, dst) in enumerate(zip(controls_hbm + (members_hbm,), owns + (members_ref,)))
    ]
    tables = [
        pltpu.make_async_copy(src, dst, load_sem.at[4 + i])
        for i, (src, dst) in enumerate(
            (
                (radii_hbm, radii_ref),
                (vertical_hbm, vertical_ref),
                (mid_picks_hbm, mid_picks_ref.at[0]),
                (coarse_picks_hbm, coarse_picks_ref.at[0]),
            )
        )
    ]
    for load in tables + loads:
        load.start()

    partners = [{"lon": before}, {"lon": after}]
    for s in shifts:
        there = lax.rem(lat + s, n_lat)
        partners += [{"lat": there}, {"lat": there, "lon": before}, {"lat": there, "lon": after}]
    for s in range(1, n_mem):
        partners.append({"mem": lax.rem(mem + s, n_mem)})
    barrier = pltpu.get_barrier_semaphore()
    for partner in partners:
        pl.semaphore_signal(barrier, inc=1, device_id=partner, device_id_type=MESH)

    starts = []
    place = 0
    for b in range(3):
        starts.append(place)
        place += count * levels * band_cols[b]
    strip_copies, corner_copies = [], []
    for b in range(3):
        loads[b].wait()
    for b in range(3):
        length = band_rows[b]
        h = iota((2 * REACH, length), 0)
        i = iota((2 * REACH, length), 1)
        edge = one_hot(i == jnp.where(h < REACH, h, length - 2 * REACH + h))
        width = count * levels * band_cols[b]
        strip_out[:, starts[b] : starts[b] + width] = dot_nt(edge, flat(owns[b][...])).astype(BF16)
        near = owns[b][...].astype(F32)
        for side in range(2):
            first = 0 if side == 0 else band_cols[b] - REACH
            part = near[:, :, first : first + REACH, :].reshape(-1, length).astype(BF16)
            packed = dot_nt(edge, part).astype(BF16)
            for m in range(count):
                lanes = levels * REACH
                corner_out[side, b * count + m] = packed[:, m * lanes : (m + 1) * lanes]
    for load in tables:
        load.wait()
    row_own, row_edge = [], []
    for b in range(3):
        radius = radii_ref[b]
        length, width = band_rows[b], band_cols[b]
        shape = (length, length)
        row_own.append(taper(radius, iota(shape, 0) - iota(shape, 1)).astype(BF16))
        shape = (2 * REACH, length)
        h, i = iota(shape, 0), iota(shape, 1)
        edge_weights = taper(radius, jnp.where(h < REACH, length + h - i, h - 2 * REACH - i))
        edges = []
        for s in shifts:
            head_ok = jnp.where(lat + 1 < n_lat, 1.0, 0.0) if s == 1 else 0.0
            tail_ok = jnp.where(lat > 0, 1.0, 0.0) if s == n_lat - 1 else 0.0
            edges.append((edge_weights * jnp.where(h < REACH, head_ok, tail_ok)).astype(BF16))
        row_edge.append(edges)

    pl.semaphore_wait(barrier, len(partners))

    def remote(src, dst, send, recv, device):
        return pltpu.make_async_remote_copy(
            src_ref=src, dst_ref=dst, send_sem=send, recv_sem=recv, device_id=device, device_id_type=MESH
        )

    def sum_copy(p, s):
        there = lax.rem(mem + s, n_mem)
        return remote(
            sum_outs[p].at[there],
            sum_ins[p].at[s - 1],
            sum_send.at[p, s - 1],
            sum_recv.at[p, s - 1],
            {"mem": there},
        )

    def start_sum(p, dest):
        @pl.when(mem != dest)
        def _():
            slot = lax.rem(dest - mem + n_mem, n_mem) - 1
            remote(
                sum_outs[p].at[dest],
                sum_ins[p].at[slot],
                sum_send.at[p, slot],
                sum_recv.at[p, slot],
                {"mem": dest},
            ).start()

    lon_copies = []
    for b in range(3):
        width = band_cols[b]
        lon_copies.append(
            remote(
                controls_hbm[b].at[:, :, width - REACH : width, :],
                sides[b].at[:, 0],
                lon_send.at[2 * b],
                lon_recv.at[2 * b],
                {"lon": after},
            )
        )
        lon_copies.append(
            remote(
                controls_hbm[b].at[:, :, 0:REACH, :],
                sides[b].at[:, 1],
                lon_send.at[2 * b + 1],
                lon_recv.at[2 * b + 1],
                {"lon": before},
            )
        )

    for k, s in enumerate(shifts):
        slot = shifts.index((n_lat - s) % n_lat)
        there = lax.rem(lat + s, n_lat)
        strip_copies.append(
            remote(strip_out, strip_in.at[slot], strip_send.at[slot], strip_recv.at[slot], {"lat": there})
        )
        for side in range(2):
            target = before if side == 0 else after
            corner_copies.append(
                remote(
                    corner_out.at[side],
                    corner_in.at[slot, :, 1 - side],
                    corner_send.at[2 * slot + side],
                    corner_recv.at[2 * slot + side],
                    {"lat": there, "lon": target},
                )
            )
    for copy in corner_copies + strip_copies + lon_copies[4:] + lon_copies[2:4] + lon_copies[:2]:
        copy.start()

    def krons(b, part):
        radius, width = radii_ref[b], band_cols[b]
        tall = levels * width
        level_of = one_hot(iota((levels, tall), 0) == (iota((levels, tall), 1) >> log2(width)))
        place_of = one_hot(iota((width, tall), 0) == (iota((width, tall), 1) & (width - 1)))
        wide = 2 * levels * REACH
        r_shift = log2(REACH)
        side_level_of = one_hot(
            iota((levels, wide), 0) == ((iota((levels, wide), 1) >> r_shift) & (levels - 1))
        )
        spot = iota((2 * REACH, wide), 1)
        spot = ((spot >> log2(levels * REACH)) << r_shift) + (spot & (REACH - 1))
        side_place_of = one_hot(iota((2 * REACH, wide), 0) == spot)
        shape = (width, width)
        own_weights = taper(radius, iota(shape, 1) - iota(shape, 0)).astype(BF16)
        shape = (width, 2 * REACH)
        c, q = iota(shape, 0), iota(shape, 1)
        side_weights = jnp.where(q < REACH, q - REACH - c, width + q - REACH - c)
        side_weights = taper(radius, side_weights).astype(BF16)
        part_width = width_of(part, width)
        tall = levels * part_width
        pick_level = one_hot((iota((tall, levels), 0) >> log2(part_width)) == iota((tall, levels), 1))
        column = column_of(part, iota((tall, width), 0) & (part_width - 1), width)
        pick_col = one_hot(column == iota((tall, width), 1))
        by_level = dot(pick_level, vertical_ref[b]).astype(BF16)

        def kron(weights, source_level, source_place):
            left = dot(by_level, source_level)
            right = dot(dot(pick_col, weights).astype(BF16), source_place)
            return (left * right).astype(BF16)

        own = kron(own_weights, level_of, place_of)
        if part == "inner":
            return own, None
        return own, kron(side_weights, side_level_of, side_place_of)

    kron = [krons(b, "all") if b else [krons(0, part) for part in parts] for b in range(3)]

    loads[3].wait()
    member_cells = flat(members_ref[...])
    group = max(1, min(levels, 256 // cols))
    restricted = [None]
    for b in (1, 2):
        factor = FACTORS[b]
        picks_ref = mid_picks_ref if b == 1 else coarse_picks_ref
        length, width = band_rows[b], band_cols[b]
        row_pick = pick_vector(picks_ref, lat * length, length, length)
        target = (iota((length, rows), 0) * factor).astype(F32) + row_pick
        by_rows = dot_nt(member_cells, one_hot(iota((length, rows), 1).astype(F32) == target)).astype(BF16)
        tall = group * width
        col_pick = pick_vector(picks_ref, n_lat * length + lon * width, tall, width)
        target = (iota((tall, group * cols), 0) * factor).astype(F32) + col_pick
        chooser = one_hot(iota((tall, group * cols), 1).astype(F32) == target)
        pieces = []
        for m in range(count):
            picked = []
            for g in range(levels // group):
                first = (m * levels + g * group) * cols
                picked.append(dot(chooser, by_rows[first : first + group * cols]))
            pieces.append(jnp.concatenate(picked, axis=0))
        restricted.append(pieces)

    own_filtered = [dot(flat(owns[b][...]), row_own[b]) for b in range(3)]
    for copy in strip_copies:
        copy.wait_recv()
    across_own = []
    for b in range(3):
        tall = levels * band_cols[b]
        across = own_filtered[b]
        for k in range(len(shifts)):
            strip = strip_in[k, :, starts[b] : starts[b] + count * tall]
            across = across + dot_tn(strip, row_edge[b][k])
        across = across.astype(BF16)
        across_own.append([across[m * tall : (m + 1) * tall] for m in range(count)])

    wide = 2 * levels * REACH

    def side_cells(b):
        for copy in lon_copies[2 * b : 2 * b + 2]:
            copy.wait_recv()
        halo = dot(flat(sides[b][...]), row_own[b])
        cells = []
        for m in range(count):
            across = halo[m * wide : (m + 1) * wide]
            for k in range(len(shifts)):
                corner = jnp.concatenate(
                    [corner_in[k, b * count + m, 0], corner_in[k, b * count + m, 1]], axis=1
                )
                across = across + dot_tn(corner, row_edge[b][k])
            cells.append(across.astype(BF16))
        return cells

    for copy in corner_copies:
        copy.wait_recv()
    spread = [None]
    for b in (1, 2):
        cells = side_cells(b)
        total = None
        for m in range(count):
            filtered = dot(kron[b][0], across_own[b][m]) + dot(kron[b][1], cells[m])
            product = restricted[b][m] * filtered
            total = product if total is None else total + product
        length = band_rows[b]
        repeat = one_hot(iota((length, rows), 0) == (iota((length, rows), 1) >> log2(FACTORS[b])))
        spread.append(dot(total.astype(BF16), repeat).astype(BF16))

    block = levels * cols // n_mem
    sum_copies = []
    for p, part in enumerate(parts):
        part_width = width_of(part, cols)
        part_block = block * part_width // cols
        kron_own, kron_side = kron[0][p]
        cells = None if part == "inner" else side_cells(0)
        fine = []
        for m in range(count):
            member = columns_of(part, members_ref[m].astype(F32))
            filtered = dot(kron_own, across_own[0][m])
            if cells is not None:
                filtered = filtered + dot(kron_side, cells[m])
            fine.append(member * filtered)
        total = fine[0]
        for product in fine[1:]:
            total = total + product
        tall = group * part_width
        dests = n_mem * group // levels
        for g in range(levels // group):
            piece = total[g * tall : (g + 1) * tall]
            for b in (1, 2):
                from_tall = group * band_cols[b]
                r = iota((tall, from_tall), 0)
                source = column_of(part, r & (part_width - 1), cols) >> log2(FACTORS[b])
                source = ((r >> log2(part_width)) << log2(band_cols[b])) + source
                repeat = one_hot(source == iota((tall, from_tall), 1))
                piece = piece + dot(repeat, spread[b][g * from_tall : (g + 1) * from_tall])
            piece = piece.reshape(-1, part_block, rows)
            here = slice(g * piece.shape[0], (g + 1) * piece.shape[0])
            field_refs[p][here] = piece
            sum_outs[p][here] = piece.astype(BF16)
            if levels // group == 1 or n_mem % (levels // group):
                continue
            for dest in range(g * dests, (g + 1) * dests):
                start_sum(p, dest)
        if levels // group == 1 or n_mem % (levels // group):
            for dest in range(n_mem):
                start_sum(p, dest)

    for p, part in enumerate(parts):
        total = field_refs[p][mem]
        for s in range(1, n_mem):
            sum_copy(p, s).wait_recv()
            total = total + sum_ins[p][s - 1].astype(F32)
        if part == "all":
            out_ref[0] = total
            continue
        total = total.reshape(block // cols, -1, rows)
        if part == "inner":
            out_ref[:, REACH : cols - REACH, :] = total
        else:
            out_ref[:, :REACH, :] = total[:, :REACH, :]
            out_ref[:, cols - REACH :, :] = total[:, REACH:, :]
    for copy in lon_copies + strip_copies + corner_copies:
        copy.wait_send()
    for p in range(len(parts)):
        for s in range(1, n_mem):
            sum_copy(p, s).wait_send()


def width_of(part, width):
    return {"inner": width - 2 * REACH, "outer": 2 * REACH, "all": width}[part]


def column_of(part, place, width):
    if part == "inner":
        return place + REACH
    if part == "outer":
        return jnp.where(place < REACH, place, place + (width - 2 * REACH))
    return place


def columns_of(part, cells):
    if part == "inner":
        cells = cells[:, REACH : cells.shape[1] - REACH, :]
    if part == "outer":
        cells = jnp.concatenate(
            [cells[:, :REACH, :], cells[:, cells.shape[1] - REACH :, :]], axis=1
        )
    return cells.reshape(-1, cells.shape[2])


def on_device(
    members,
    control_fine,
    control_mid,
    control_coarse,
    vertical,
    mid_picks,
    coarse_picks,
    band_radii,
):
    n_mem, n_lat, n_lon = (lax.axis_size(axis) for axis in ("mem", "lat", "lon"))
    shifts = sorted({1, n_lat - 1}) if n_lat > 1 else []
    slots = max(1, len(shifts))
    count, levels, cols, rows = members.shape
    controls = (control_fine, control_mid, control_coarse)
    block = levels * cols // n_mem
    inner = cols - 2 * REACH
    split = block % cols == 0 and inner > 0 and inner & (inner - 1) == 0
    parts = ("inner", "outer") if split else ("all",)
    out_shape = (block // cols, cols, rows) if split else (1, block, rows)
    strip_lanes = sum(count * levels * c.shape[2] for c in controls)
    corner_lanes = levels * REACH
    hbm_spec = pl.BlockSpec(memory_space=pltpu.HBM)
    vmem_spec = pl.BlockSpec(memory_space=pltpu.VMEM)
    dma = pltpu.SemaphoreType.DMA
    scratch = (
        [
            pltpu.VMEM(vertical.shape, BF16),
            pltpu.VMEM((1,) + mid_picks.shape, jnp.int32),
            pltpu.VMEM((1,) + coarse_picks.shape, jnp.int32),
            pltpu.SMEM(band_radii.shape, jnp.int32),
            pltpu.VMEM(members.shape, BF16),
        ]
        + [pltpu.VMEM(c.shape, BF16) for c in controls]
        + [pltpu.VMEM((count, 2, levels, REACH, c.shape[3]), BF16) for c in controls]
        + [
            pltpu.VMEM((2 * REACH, strip_lanes), BF16),
            pltpu.VMEM((slots, 2 * REACH, strip_lanes), BF16),
            pltpu.VMEM((2, 3 * count, 2 * REACH, corner_lanes), BF16),
            pltpu.VMEM((slots, 3 * count, 2, 2 * REACH, corner_lanes), BF16),
        ]
        + [pltpu.VMEM((n_mem, block * width_of(p, cols) // cols, rows), F32) for p in parts]
        + [pltpu.VMEM((n_mem, block * width_of(p, cols) // cols, rows), BF16) for p in parts] * 2
        + [
            dma((8,)),
            dma((6,)),
            dma((6,)),
            dma((slots,)),
            dma((slots,)),
            dma((2 * slots,)),
            dma((2 * slots,)),
            dma((len(parts), n_mem)),
            dma((len(parts), n_mem)),
        ]
    )
    summed = pl.pallas_call(
        functools.partial(kernel, (n_mem, n_lat, n_lon, shifts, parts)),
        out_shape=jax.ShapeDtypeStruct(out_shape, F32),
        in_specs=[hbm_spec] * 8,
        out_specs=vmem_spec,
        scratch_shapes=scratch,
        compiler_params=pltpu.CompilerParams(
            collective_id=0, has_side_effects=True, vmem_limit_bytes=67043328
        ),
    )(
        *((members,) + controls),
        vertical,
        mid_picks,
        coarse_picks,
        band_radii,
    )
    scale = 1.0 / math.sqrt(count * n_mem - 1)
    return (summed * scale).reshape(1, block, rows)


def solution(mesh):
    placed = (
        P("mem", None, "lon", "lat"),
        P("mem", None, "lon", "lat"),
        P("mem", None, "lon", "lat"),
        P("mem", None, "lon", "lat"),
        P(),
        P(),
        P(),
        P(),
    )
    return jax.shard_map(
        on_device, mesh=mesh, in_specs=placed, out_specs=P("lon", "mem", "lat"), check_vma=False
    )
```
